512 devices in a mesh: stn: 64 (over x, y, z_hi, core), chan: 8 (over z_lo).
Axes of the slice: x: 4, y: 4, z: 16 (z_hi: 2, z_lo: 8; z = z_hi * 8 + z_lo), core: 2. Of those that a mesh axis runs over, the one named last changes fastest.
Arguments:
- voltages: bfloat16 [512, 2, 2, 8, 4864], P('stn', None, None, 'chan'), may hold values from -6 to 6
- prototype: float32 [16, 256], replicated, may hold values from -1.5 to 1.5
- kernel_table: float32 [8, 7], replicated, may hold values from 0.05 to 1
- tile_subgrid: int32 [8, 512, 4, 512, 1], P('chan', 'stn'), may hold values from 0 to 31; in each aligned block of 16384 rows (0 to 16383, 16384 to 32767, ..., all dimensions but the last counted through in order) at most 1024 rows name the same one
- tile_cells: int32 [8, 512, 4, 512, 2], P('chan', 'stn'), may hold values from 3 to 44
- tile_offsets: int32 [8, 512, 4, 512, 2], P('chan', 'stn'), may hold values from 0 to 7
- subgrid_slot: int32 [32], replicated, may hold values from 0 to 31, each once
Outputs:
- uv_grid: float32 [32, 48, 384], P('chan', None, 'stn')
The draws below stay inside these ranges and needn't reach their ends.
Inputs may be any that keep to these rules, and one draw needn't show every extreme that they name: `tile_subgrid`: among the tiles of one device (one coarse channel c and the 8 stations a of one index of stn), no subgrid is named more than 1024 times, and in every draw some device's tiles name some subgrid exactly 1024 times. `subgrid_slot`: each of 0 to 31 appears once.
All inputs are finite; a program needn't handle non-finite values.
Results may differ from the reference program's by a relative error of at most 0.0066.
Values may be sent and summed in bfloat16 or wider, within the bound.
No kernel may reach another device: no remote copies, remote signals or barrier semaphores. Data moves between devices by JAX's collectives and lax.ppermute only.
A program may use at most 128 MiB of HBM per device.

```python
import math
import jax
import jax.numpy as jnp
import numpy as np
from jax import lax

FINE = 256
TAPS = 16
FRAMES = 4
CT = 4
CB = 64
STN_DEV = 8
STATIONS = 512
G = 48
NSUB = 32
KW = 7
OS = 8
SAMPLES = 4864
TILES_DEV = 16384
MOST = 1024
N_STN = 64
N_CHAN = 8


def plant(values, own_key, smallest, high):
    dims = values.shape
    place = [jax.random.randint(jax.random.fold_in(own_key, axis), (), 0, dims[axis]) for axis in range(len(dims))]
    values = values.at[tuple(place)].set(smallest)
    longest = dims.index(max(dims))
    place[longest] = (place[longest] + 1) % dims[longest]
    return values.at[tuple(place)].set(high)


def block_levels(key, shape, shards, least, largest):
    def one(axis_at, shards_of):
        steps = jax.random.uniform(jax.random.fold_in(jax.random.fold_in(key, 6), axis_at), (shards_of,), jnp.float32, least / len(shards), largest / len(shards))
        return jnp.repeat(jnp.exp(steps), shape[axis_at] // shards_of).reshape((-1,) + (1,) * (len(shape) - axis_at - 1))

    gain = one(*shards[0])
    for cut in shards[1:]:
        gain = gain * one(*cut)
    return gain


def routed_block(key, own, number, rows, amount, top, limit, skew):
    ranking = jax.random.permutation(key, amount)
    heavy_load, ordinary = portions_of(amount, rows * top, limit, skew, True), portions_of(amount, rows * top, limit, skew, False)
    places = jnp.arange(amount)

    def named(sizes, turn):
        used = int((sizes > 0).sum())
        fixed = max(1, used // 4)
        passed = fixed + (places - fixed + turn * (used - fixed)) % max(1, amount - fixed)
        return jnp.zeros((amount,), jnp.int32).at[ranking[jnp.where(places < fixed, places, passed)]].set(jnp.asarray(sizes, jnp.int32))

    sizes = jnp.where(number % 4 == 0, named(heavy_load, number // 4), named(ordinary, number - number // 4 - 1))
    mixed = jax.random.permutation(jax.random.fold_in(own, 3), amount)
    source_of, taker = mixed[0:amount // 2 * 2:2], mixed[1:amount // 2 * 2:2]
    slack = jnp.minimum(sizes[source_of] - 1, limit - sizes[taker]) // 2
    slack = jnp.where((source_of == ranking[0]) | (taker == ranking[0]) | (sizes[taker] == 0), 0, jnp.maximum(slack, 0))
    passed = jax.random.randint(jax.random.fold_in(own, 4), (amount // 2,), 0, 1 << 20) % (slack + 1)
    sizes = sizes.at[source_of].add(-passed).at[taker].add(passed)
    items = jnp.searchsorted(jnp.cumsum(sizes), jnp.arange(rows * top), side="right").astype(jnp.int32)
    grid = items.reshape(top, rows).T
    grid = grid[jax.random.permutation(jax.random.fold_in(own, 1), rows)]
    turn = jax.random.randint(jax.random.fold_in(own, 2), (rows, 1), 0, top)
    return jnp.take_along_axis(grid, (jnp.arange(top)[None, :] + turn) % top, axis=1)


def portions_of(count, total, bound, lean, full):
    portions = [(1 << 20) // math.isqrt(grade ** lean) + 1 for grade in range(1, count + 1)]
    largest = bound if full else min(bound, max(-(-total // count), total * portions[0] // sum(portions)))
    least = 1 if total - largest >= count - 1 else 0
    holding, surplus = [largest] + [least] * (count - 1), total - largest - least * (count - 1)
    while surplus > 0:
        movable = [i for i in range(1, count) if holding[i] < largest] or [i for i in range(1, count) if holding[i] < bound]
        whole, budget = sum([portions[i] for i in movable]), surplus
        for i in movable:
            addition = min(bound - holding[i], max(1, budget * portions[i] // whole), surplus)
            holding[i] = holding[i] + addition
            surplus = surplus - addition
    return np.array(holding)


def normal_values(stream_key, extent, spread, reach, pieces=(), kind=jnp.bfloat16):
    result = jax.random.normal(stream_key, extent, jnp.float32) * spread
    if len(pieces) > 0:
        result = block_levels(stream_key, extent, pieces, -0.22, 0.18) * result
    return jnp.clip(result, min=-reach, max=reach).astype(kind)


def setup_inputs(seed: int = 0) -> dict:
    streams_of = jax.random.split(jax.random.key(seed), 8)
    voltages = normal_values(streams_of[0], (STATIONS, 2, 2, N_CHAN, SAMPLES), 1.0, 6.0, ((0, 64), (3, 8)))
    prototype = normal_values(streams_of[1], (TAPS, FINE), TAPS ** -0.5, 1.5, (), jnp.float32)
    kernel_table = jnp.clip(jax.random.uniform(streams_of[2], (OS, KW), jnp.float32, 0.05, 1.0), 0.05, 1.0)
    tile_subgrid_keys = jax.random.split(jax.random.fold_in(streams_of[3], 1), N_CHAN * STATIONS * CT * STATIONS // TILES_DEV)
    tile_subgrid_turns = jax.random.permutation(jax.random.fold_in(streams_of[3], 3), N_CHAN * STATIONS * CT * STATIONS // TILES_DEV)
    tile_subgrid = jax.vmap(lambda own, number: routed_block(jax.random.fold_in(streams_of[3], 2), own, number, TILES_DEV, NSUB, 1, MOST, 1))(tile_subgrid_keys, tile_subgrid_turns).reshape((N_CHAN, STATIONS, CT, STATIONS, 1))
    tile_cells = plant(jax.random.randint(streams_of[4], (N_CHAN, STATIONS, CT, STATIONS, 2), 3, G - 3), jax.random.fold_in(streams_of[4], 1), 3, (G - 3) - 1).astype(jnp.int32)
    tile_offsets = plant(jax.random.randint(streams_of[5], (N_CHAN, STATIONS, CT, STATIONS, 2), 0, OS), jax.random.fold_in(streams_of[5], 1), 0, OS - 1).astype(jnp.int32)
    subgrid_slot = jax.random.permutation(streams_of[6], NSUB).astype(jnp.int32)
    return dict(voltages=voltages, prototype=prototype, kernel_table=kernel_table, tile_subgrid=tile_subgrid, tile_cells=tile_cells, tile_offsets=tile_offsets, subgrid_slot=subgrid_slot)


def place_taps(taps, centre, width):
    cells = jnp.arange(width, dtype=jnp.int32)
    placed = jnp.zeros((taps.shape[0], width), jnp.float32)
    for offset in range(KW):
        hit = cells[None, :] == centre[:, None] + (offset - KW // 2)
        placed = jnp.where(hit, taps[:, offset:offset + 1].astype(jnp.float32), placed)
    return placed

def grid_bucket(payload, cells):
    values = payload[:, :8].astype(jnp.float32)
    across = place_taps(payload[:, 8:8 + KW], cells[:, 0], G)
    down = place_taps(payload[:, 8 + KW:8 + 2 * KW], cells[:, 1], G).astype(jnp.bfloat16)
    weighted = (values[:, :, None] * across[:, None, :]).astype(jnp.bfloat16)
    weighted = weighted.reshape(payload.shape[0], 8 * G)
    return jnp.dot(down.T, weighted, preferred_element_type=jnp.float32)

def grid_pair(pair):
    return grid_bucket(pair[0], pair[1])

def reference(voltages, prototype, kernel_table, tile_subgrid, tile_cells, tile_offsets, subgrid_slot):
    samples = voltages.astype(jnp.float32).reshape(STATIONS, 2, 2, N_CHAN, FRAMES + TAPS - 1, FINE)
    filtered = jnp.zeros((STATIONS, 2, 2, N_CHAN, FRAMES, FINE), jnp.float32)
    for tap in range(TAPS):
        filtered = filtered + prototype[tap] * samples[:, :, :, :, tap:tap + FRAMES, :]
    spectrum = jnp.fft.fft(lax.complex(filtered[:, :, 0], filtered[:, :, 1]), axis=-1) / math.sqrt(FINE)
    real_part = jnp.real(spectrum).astype(jnp.bfloat16)
    imag_part = jnp.imag(spectrum).astype(jnp.bfloat16)
    stacked = jnp.stack([real_part, imag_part], axis=2)
    stacked = stacked.reshape(STATIONS, 2, 2, N_CHAN, FRAMES, CT, CB)
    signals = stacked.transpose(3, 5, 0, 1, 2, 4, 6).reshape(N_CHAN, CT, 2 * STATIONS, 2 * FRAMES * CB)
    halfway = FRAMES * CB
    autos = 1.0 - jnp.eye(STATIONS, dtype=jnp.float32)

    def one_tile(rows):
        flipped = jnp.concatenate([-rows[:, halfway:], rows[:, :halfway]], axis=1)
        real_sum = jnp.dot(rows, rows.T, preferred_element_type=jnp.float32)
        imag_sum = jnp.dot(rows, flipped.T, preferred_element_type=jnp.float32)
        both = jnp.stack([real_sum, imag_sum], 0).reshape(2, STATIONS, 2, STATIONS, 2)
        both = both.transpose(1, 3, 0, 2, 4).reshape(STATIONS, STATIONS, 8)
        return both * (1.0 / halfway) * autos[:, :, None]

    def correlate_channel(block):
        tiles_now = lax.map(one_tile, block)
        return tiles_now.transpose(1, 0, 2, 3).astype(jnp.bfloat16)
    visibilities = lax.map(correlate_channel, signals)
    zero = jnp.zeros((), jnp.int32)

    def grid_block(total, number):
        channel = (number // N_STN).astype(jnp.int32)
        station = (number % N_STN * STN_DEV).astype(jnp.int32)
        start = (channel, station, zero, zero, zero)
        values = lax.dynamic_slice(visibilities, start, (1, STN_DEV, CT, STATIONS, 8)).reshape(TILES_DEV, 8)
        subgrid = lax.dynamic_slice(tile_subgrid, start, (1, STN_DEV, CT, STATIONS, 1)).reshape(TILES_DEV)
        cells = lax.dynamic_slice(tile_cells, start, (1, STN_DEV, CT, STATIONS, 2)).reshape(TILES_DEV, 2)
        offsets = lax.dynamic_slice(tile_offsets, start, (1, STN_DEV, CT, STATIONS, 2)).reshape(TILES_DEV, 2)
        position = subgrid_slot[subgrid]
        member = (position[:, None] == jnp.arange(NSUB, dtype=jnp.int32)[None, :]).astype(jnp.int32)
        rank = lax.optimization_barrier(jnp.sum(member * jnp.cumsum(member, axis=0), axis=1)) - 1
        target = position * MOST + rank
        across = kernel_table[offsets[:, 0]].astype(jnp.bfloat16)
        down = kernel_table[offsets[:, 1]].astype(jnp.bfloat16)
        payload = jnp.concatenate([values, across, down], axis=1)
        slots = jnp.zeros((NSUB * MOST, 8 + 2 * KW), jnp.bfloat16).at[target].set(payload)
        places = jnp.zeros((NSUB * MOST, 2), jnp.int32).at[target].set(cells)
        grids = lax.map(grid_pair, (slots.reshape(NSUB, MOST, 8 + 2 * KW), places.reshape(NSUB, MOST, 2)))
        return (total + grids, None)
    total, unused = lax.scan(grid_block, jnp.zeros((NSUB, G, 8 * G), jnp.float32), jnp.arange(N_CHAN * N_STN, dtype=jnp.int32))
    return total
```

```python
import math

import jax
import jax.numpy as jnp
from jax import lax
from jax.experimental import pallas as pl
from jax.experimental.pallas import tpu as pltpu
from jax.sharding import Mesh, PartitionSpec as P

FINE = 256
TAPS = 16
FRAMES = 4
CT = 4
CB = FINE // CT
STN_DEV = 8
STATIONS = 512
G = 48
NSUB = 32
KW = 7
OS = 8
SIDE = 768
STN = ("x", "y", "zh", "core")


def fourier_table(length):
    index = jnp.arange(length, dtype=jnp.int32)
    phase = index[:, None] * index[None, :] % length
    angle = phase.astype(jnp.float32) * (2.0 * math.pi / length)
    cosine = jnp.cos(angle) / math.sqrt(length)
    sine = jnp.sin(angle) / math.sqrt(length)
    upper = jnp.concatenate([cosine, -sine], axis=1)
    lower = jnp.concatenate([sine, cosine], axis=1)
    return jnp.concatenate([upper, lower], axis=0)


def channelize(voltages, prototype):
    stations = voltages.shape[0]
    samples = (
        voltages[:, :, :, 0, :].astype(jnp.float32).reshape(stations, 2, 2, FRAMES + TAPS - 1, FINE)
    )
    filtered = jnp.zeros((stations, 2, 2, FRAMES, FINE), jnp.float32)
    for tap in range(TAPS):
        filtered = filtered + prototype[tap] * samples[:, :, :, tap : tap + FRAMES, :]
    frame_rows = filtered.transpose(0, 1, 3, 2, 4).reshape(stations * 2 * FRAMES, 2 * FINE)
    spectra = jnp.dot(frame_rows, fourier_table(FINE), precision=lax.Precision.HIGHEST).astype(
        jnp.bfloat16
    )
    spectra = spectra.reshape(stations, 2, FRAMES, 2, CT, CB)
    return spectra.transpose(4, 1, 0, 3, 2, 5).reshape(CT, 2, stations, 2 * FRAMES * CB)


def grid_body(table, index, urow, lhs, rhs, send, keep, vis, taps, amat, wmat):
    step = pl.program_id(0)

    @pl.when(step == 0)
    def _():
        send[...] = jnp.zeros_like(send)
        keep[...] = jnp.zeros_like(keep)

    product = lax.dot_general(
        lhs[0], rhs[0], (((1,), (1,)), ((), ())), preferred_element_type=jnp.float32
    )
    product = (product * (1.0 / (FRAMES * CB))).astype(jnp.bfloat16).astype(jnp.float32)
    vis[...] = product.reshape(4, STN_DEV, 2 * STATIONS)
    for axis in range(2):
        chosen = index[0, 3 + axis]
        masks = [chosen == o for o in range(1, OS)]
        for k in range(KW):
            value = jnp.full((STN_DEV, STATIONS), table[0, k], jnp.float32)
            for o in range(1, OS):
                value = jnp.where(masks[o - 1], table[o, k], value)
            taps[axis * KW + k] = value

    def one_station(a, carry):
        row = pl.ds(a, 1)
        position = index[0, 0, row, :]
        u0 = index[0, 1, row, :] + 64 * (position & 1) - KW // 2
        v0 = index[0, 2, row, :] - KW // 2
        high = position >> 1
        shape = (G, STATIONS)
        away = lax.broadcasted_iota(jnp.int32, shape, 0) - v0
        down = jnp.zeros(shape, jnp.float32)
        for k in range(KW):
            down = jnp.where(away == k, taps[KW + k, row, :], down)
        for h in range(NSUB // 2):
            amat[h * G : (h + 1) * G, :] = jnp.where(high == h, down, 0.0).astype(jnp.bfloat16)
        for half in range(2):
            away = urow[half * G : (half + 1) * G, :] - u0
            across = jnp.zeros(shape, jnp.float32)
            for k in range(KW):
                across = jnp.where(away == k, taps[k, row, :], across)
            for j in range(8):
                value = vis[j // 2, row, (j % 2) * STATIONS : (j % 2 + 1) * STATIONS]
                first = half * 8 * G + j * G
                wmat[first : first + G, :] = (value * across).astype(jnp.bfloat16)
        nt = (((1,), (1,)), ((), ()))
        total = lax.dot_general(
            wmat[...], amat[...], nt, preferred_element_type=jnp.float32
        )
        send[...] += total[: SIDE // 2]
        keep[...] += total[SIDE // 2 :]
        return carry

    lax.fori_loop(0, STN_DEV, one_station, 0)


def grid_tiles(table, index, urow, lhs, rhs):
    half = jax.ShapeDtypeStruct((SIDE // 2, SIDE), jnp.float32)
    whole = pl.BlockSpec((SIDE // 2, SIDE), lambda t: (0, 0))
    return pl.pallas_call(
        grid_body,
        grid=(CT,),
        in_specs=[
            pl.BlockSpec(memory_space=pltpu.SMEM),
            pl.BlockSpec((1, 5, STN_DEV, STATIONS), lambda t: (t, 0, 0, 0)),
            pl.BlockSpec((2 * G, STATIONS), lambda t: (0, 0)),
            pl.BlockSpec((1, 4 * STN_DEV, 2 * FRAMES * CB), lambda t: (t, 0, 0)),
            pl.BlockSpec((1, 2 * STATIONS, 2 * FRAMES * CB), lambda t: (t, 0, 0)),
        ],
        out_specs=[whole, whole],
        out_shape=[half, half],
        scratch_shapes=[
            pltpu.VMEM((4, STN_DEV, 2 * STATIONS), jnp.float32),
            pltpu.VMEM((2 * KW, STN_DEV, STATIONS), jnp.float32),
            pltpu.VMEM((SIDE, STATIONS), jnp.bfloat16),
            pltpu.VMEM((SIDE, STATIONS), jnp.bfloat16),
        ],
    )(table, index, urow, lhs, rhs)


def per_device(
    voltages, prototype, kernel_table, tile_subgrid, tile_cells, tile_offsets, subgrid_slot
):
    spectra = channelize(voltages, prototype)
    theirs = lax.all_gather(spectra, STN, axis=2, tiled=True).reshape(
        CT, 2 * STATIONS, 2 * FRAMES * CB
    )
    lanes = FRAMES * CB
    turned = jnp.concatenate([spectra[..., lanes:], -spectra[..., :lanes]], axis=-1)
    lhs = jnp.stack([spectra, turned], axis=1).reshape(CT, 4 * STN_DEV, 2 * lanes)

    core = lax.axis_index("core")
    subgrid = tile_subgrid.reshape(STN_DEV, CT, STATIONS)
    places = jnp.arange(NSUB, dtype=jnp.int32)
    position = jnp.sum(
        jnp.where(subgrid[..., None] == places, subgrid_slot, 0), axis=-1
    )
    mine = lax.axis_index(STN) * STN_DEV + jnp.arange(STN_DEV, dtype=jnp.int32)
    station = jnp.arange(STATIONS, dtype=jnp.int32)
    position = jnp.where(mine[:, None, None] == station, -1, position)
    cells = tile_cells.reshape(STN_DEV, CT, STATIONS, 2)
    offsets = tile_offsets.reshape(STN_DEV, CT, STATIONS, 2)
    index = jnp.stack(
        [position, cells[..., 0], cells[..., 1], offsets[..., 0], offsets[..., 1]], axis=0
    ).transpose(2, 0, 1, 3)
    r = jnp.arange(G, dtype=jnp.int32)
    base = (r // 24) * 24 + (r // 12) % 2 * 12 + r % 6 + 64 * ((r // 6) % 2)
    urow = jnp.concatenate([base + 6 * (1 - core), base + 6 * core])
    urow = jnp.broadcast_to(urow[:, None], (2 * G, STATIONS))
    table = lax.reduce_precision(kernel_table, 8, 7)

    send, keep = grid_tiles(table, index, urow, lhs, theirs)
    total = keep + lax.ppermute(send, "core", [(0, 1), (1, 0)])
    for axis in ("x", "y"):
        total = total.reshape(4, -1, SIDE)
        total = jnp.sum(lax.all_to_all(total, axis, 0, 0, tiled=True), axis=0)
    total = total.reshape(2, 12, 8, 96).transpose(0, 2, 1, 3).reshape(16, 12, 96)
    total = jnp.sum(lax.all_to_all(total, ("zh", "chan"), 0, 0, tiled=True), axis=0)
    total = total.reshape(2, 6, 2, G)
    return total.transpose(2, 0, 3, 1).reshape(4, G, 6)


def solution(mesh):
    fine = Mesh(mesh.devices.reshape(4, 4, 2, 2, 8), STN + ("chan",))
    return jax.shard_map(
        per_device,
        mesh=fine,
        in_specs=(
            P(STN, None, None, "chan", None),
            P(),
            P(),
            P("chan", STN, None, None, None),
            P("chan", STN, None, None, None),
            P("chan", STN, None, None, None),
            P(),
        ),
        out_specs=P("chan", None, STN),
        check_vma=False,
    )
```

```python
import math

import jax
import jax.numpy as jnp
from jax import lax
from jax.experimental import pallas as pl
from jax.experimental.pallas import tpu as pltpu
from jax.sharding import Mesh, PartitionSpec as P

FINE = 256
TAPS = 16
FRAMES = 4
CT = 4
CB = FINE // CT
STN_DEV = 8
STATIONS = 512
G = 48
NSUB = 32
KW = 7
OS = 8
SIDE = 768
PART = 256
BUNCH = 2
STN = ("x", "y", "zh", "core")


def fourier_table(length):
    index = jnp.arange(length, dtype=jnp.int32)
    phase = index[:, None] * index[None, :] % length
    angle = phase.astype(jnp.float32) * (2.0 * math.pi / length)
    cosine = jnp.cos(angle) / math.sqrt(length)
    sine = jnp.sin(angle) / math.sqrt(length)
    upper = jnp.concatenate([cosine, -sine], axis=1)
    lower = jnp.concatenate([sine, cosine], axis=1)
    return jnp.concatenate([upper, lower], axis=0)


def channelize(voltages, prototype):
    stations = voltages.shape[0]
    samples = (
        voltages[:, :, :, 0, :].astype(jnp.float32).reshape(stations, 2, 2, FRAMES + TAPS - 1, FINE)
    )
    filtered = jnp.zeros((stations, 2, 2, FRAMES, FINE), jnp.float32)
    for tap in range(TAPS):
        filtered = filtered + prototype[tap] * samples[:, :, :, tap : tap + FRAMES, :]
    frame_rows = filtered.transpose(0, 1, 3, 2, 4).reshape(stations * 2 * FRAMES, 2 * FINE)
    spectra = jnp.dot(frame_rows, fourier_table(FINE), precision=lax.Precision.HIGHEST).astype(
        jnp.bfloat16
    )
    spectra = spectra.reshape(stations, 2, FRAMES, 2, CT, CB)
    return spectra.transpose(4, 1, 0, 3, 2, 5).reshape(CT, 2, stations, 2 * FRAMES * CB)


def grid_body(
    table, index, urow, lhs, near, far, send_in, keep_in, send, keep, vis, taps, amat, wmat
):
    step = pl.program_id(0)

    @pl.when(step == 0)
    def _():
        send[...] = send_in[...]
        keep[...] = keep_in[...]

    width = PART // 2
    for side, rhs in enumerate((near, far)):
        product = lax.dot_general(
            lhs[0], rhs[0], (((1,), (1,)), ((), ())), preferred_element_type=jnp.float32
        )
        product = (product * (1.0 / (FRAMES * CB))).astype(jnp.bfloat16).astype(jnp.float32)
        product = product.reshape(4, STN_DEV, 2 * width)
        for q in range(2):
            first = q * PART + side * width
            vis[:, :, first : first + width] = product[:, :, q * width : (q + 1) * width]
    for axis in range(2):
        chosen = index[0, 3 + axis]
        masks = [chosen == o for o in range(1, OS)]
        for k in range(KW):
            value = jnp.full((STN_DEV, PART), table[0, k], jnp.float32)
            for o in range(1, OS):
                value = jnp.where(masks[o - 1], table[o, k], value)
            taps[axis * KW + k] = value

    def stations(turn, carry):
        for inner in range(BUNCH):
            row = pl.ds(turn * BUNCH + inner, 1)
            lanes = slice(inner * PART, (inner + 1) * PART)
            position = index[0, 0, row, :]
            u0 = index[0, 1, row, :] + 64 * (position & 1) - KW // 2
            v0 = index[0, 2, row, :] - KW // 2
            high = position >> 1
            shape = (G, PART)
            away = lax.broadcasted_iota(jnp.int32, shape, 0) - v0
            down = jnp.zeros(shape, jnp.float32)
            for k in range(KW):
                down = jnp.where(away == k, taps[KW + k, row, :], down)
            for h in range(NSUB // 2):
                amat[h * G : (h + 1) * G, lanes] = jnp.where(high == h, down, 0.0).astype(
                    jnp.bfloat16
                )
            for half in range(2):
                away = urow[half * G : (half + 1) * G, :] - u0
                across = jnp.zeros(shape, jnp.float32)
                for k in range(KW):
                    across = jnp.where(away == k, taps[k, row, :], across)
                for j in range(8):
                    value = vis[j // 2, row, (j % 2) * PART : (j % 2 + 1) * PART]
                    first = half * 8 * G + j * G
                    wmat[first : first + G, lanes] = (value * across).astype(jnp.bfloat16)
        total = lax.dot_general(
            wmat[...], amat[...], (((1,), (1,)), ((), ())), preferred_element_type=jnp.float32
        )
        send[...] += total[: SIDE // 2]
        keep[...] += total[SIDE // 2 :]
        return carry

    lax.fori_loop(0, STN_DEV // BUNCH, stations, 0)


def grid_tiles(table, index, urow, lhs, near, far, send, keep, part):
    half = jax.ShapeDtypeStruct((SIDE // 2, SIDE), jnp.float32)
    whole = pl.BlockSpec((SIDE // 2, SIDE), lambda t: (0, 0))
    lanes = 2 * FRAMES * CB
    piece = pl.BlockSpec((1, PART, lanes), lambda t: (t, 0, 0))
    return pl.pallas_call(
        grid_body,
        grid=(CT,),
        in_specs=[
            pl.BlockSpec(memory_space=pltpu.SMEM),
            pl.BlockSpec((1, 5, STN_DEV, PART), lambda t: (t, 0, 0, part)),
            pl.BlockSpec((2 * G, PART), lambda t: (0, 0)),
            pl.BlockSpec((1, 4 * STN_DEV, lanes), lambda t: (t, 0, 0)),
            piece,
            piece,
            whole,
            whole,
        ],
        out_specs=[whole, whole],
        out_shape=[half, half],
        input_output_aliases={6: 0, 7: 1},
        scratch_shapes=[
            pltpu.VMEM((4, STN_DEV, 2 * PART), jnp.float32),
            pltpu.VMEM((2 * KW, STN_DEV, PART), jnp.float32),
            pltpu.VMEM((SIDE, BUNCH * PART), jnp.bfloat16),
            pltpu.VMEM((SIDE, BUNCH * PART), jnp.bfloat16),
        ],
    )(table, index, urow, lhs, near, far, send, keep)


def spread_over_plane(spectra):
    copies = jnp.broadcast_to(spectra, (16,) + spectra.shape)
    pieces = lax.all_to_all(copies, ("x", "y"), 0, 0, tiled=True)
    near = pieces.transpose(1, 2, 0, 3, 4).reshape(CT, PART, 2 * FRAMES * CB)
    return near, lax.ppermute(near, "core", [(0, 1), (1, 0)])


def arrival_order():
    slot = jnp.arange(STATIONS, dtype=jnp.int32)
    zh = lax.axis_index("zh") ^ (slot // 256)
    core = lax.axis_index("core") ^ (slot // 128 % 2)
    return ((slot // 8 % 16) * 4 + zh * 2 + core) * STN_DEV + slot % 8


def per_device(
    voltages, prototype, kernel_table, tile_subgrid, tile_cells, tile_offsets, subgrid_slot
):
    swap = [(0, 1), (1, 0)]
    spectra = channelize(voltages, prototype)
    other = lax.ppermute(spectra, "zh", swap)
    parts = (spread_over_plane(spectra), spread_over_plane(other))
    lanes = FRAMES * CB
    turned = jnp.concatenate([spectra[..., lanes:], -spectra[..., :lanes]], axis=-1)
    lhs = jnp.stack([spectra, turned], axis=1).reshape(CT, 4 * STN_DEV, 2 * lanes)

    core = lax.axis_index("core")
    subgrid = tile_subgrid.reshape(STN_DEV, CT, STATIONS)
    places = jnp.arange(NSUB, dtype=jnp.int32)
    position = jnp.sum(
        jnp.where(subgrid[..., None] == places, subgrid_slot, 0), axis=-1
    )
    mine = lax.axis_index(STN) * STN_DEV + jnp.arange(STN_DEV, dtype=jnp.int32)
    station = jnp.arange(STATIONS, dtype=jnp.int32)
    position = jnp.where(mine[:, None, None] == station, -1, position)
    cells = tile_cells.reshape(STN_DEV, CT, STATIONS, 2)
    offsets = tile_offsets.reshape(STN_DEV, CT, STATIONS, 2)
    index = jnp.stack(
        [position, cells[..., 0], cells[..., 1], offsets[..., 0], offsets[..., 1]], axis=0
    ).transpose(2, 0, 1, 3)
    chosen = (station[:, None] == arrival_order()[None, :]).astype(jnp.bfloat16)
    index = jnp.dot(
        index.reshape(-1, STATIONS).astype(jnp.bfloat16),
        chosen,
        preferred_element_type=jnp.float32,
    )
    index = index.astype(jnp.int32).reshape(CT, 5, STN_DEV, STATIONS)
    r = jnp.arange(G, dtype=jnp.int32)
    base = (r // 24) * 24 + (r // 12) % 2 * 12 + r % 6 + 64 * ((r // 6) % 2)
    urow = jnp.concatenate([base + 6 * (1 - core), base + 6 * core])
    urow = jnp.broadcast_to(urow[:, None], (2 * G, PART))
    table = lax.reduce_precision(kernel_table, 8, 7)

    send = jnp.zeros((SIDE // 2, SIDE), jnp.float32)
    keep = jnp.zeros((SIDE // 2, SIDE), jnp.float32)
    for part, (near, far) in enumerate(parts):
        send, keep = grid_tiles(table, index, urow, lhs, near, far, send, keep, part)
    total = keep + lax.ppermute(send.astype(jnp.bfloat16), "core", swap).astype(jnp.float32)
    total = total.astype(jnp.bfloat16).reshape(16, 24, SIDE)
    total = lax.all_to_all(total, ("x", "y"), 0, 0, tiled=True)
    total = jnp.sum(total.astype(jnp.float32), axis=0)
    total = total.reshape(2, 12, 8, 96).transpose(0, 2, 1, 3).reshape(16, 12, 96)
    total = jnp.sum(lax.all_to_all(total, ("zh", "chan"), 0, 0, tiled=True), axis=0)
    total = total.reshape(2, 6, 2, G)
    return total.transpose(2, 0, 3, 1).reshape(4, G, 6)


def solution(mesh):
    fine = Mesh(mesh.devices.reshape(4, 4, 2, 2, 8), STN + ("chan",))
    return jax.shard_map(
        per_device,
        mesh=fine,
        in_specs=(
            P(STN, None, None, "chan", None),
            P(),
            P(),
            P("chan", STN, None, None, None),
            P("chan", STN, None, None, None),
            P("chan", STN, None, None, None),
            P(),
        ),
        out_specs=P("chan", None, STN),
        check_vma=False,
    )
```

```python
import math

import jax
import jax.numpy as jnp
import numpy as np
from jax import lax
from jax.experimental import pallas as pl
from jax.experimental.pallas import tpu as pltpu
from jax.sharding import Mesh, PartitionSpec as P

FINE = 256
TAPS = 16
FRAMES = 4
CT = 4
CB = FINE // CT
STN_DEV = 8
STATIONS = 512
G = 48
NSUB = 32
KW = 7
OS = 8
SIDE = 768
PART = 128
BUNCH = 4
STN = ("x", "y", "zh", "core")


def fourier_table(length):
    index = np.arange(length)
    angle = (index[:, None] * index[None, :] % length) * (2.0 * math.pi / length)
    cosine = np.cos(angle) / math.sqrt(length)
    sine = np.sin(angle) / math.sqrt(length)
    upper = np.concatenate([cosine, -sine], axis=1)
    lower = np.concatenate([sine, cosine], axis=1)
    return np.concatenate([upper, lower], axis=0).astype(np.float32)


def channelize(voltages, prototype):
    stations = voltages.shape[0]
    samples = (
        voltages[:, :, :, 0, :].astype(jnp.float32).reshape(stations, 2, 2, FRAMES + TAPS - 1, FINE)
    )
    filtered = jnp.zeros((stations, 2, 2, FRAMES, FINE), jnp.float32)
    for tap in range(TAPS):
        filtered = filtered + prototype[tap] * samples[:, :, :, tap : tap + FRAMES, :]
    frame_rows = filtered.transpose(0, 1, 3, 2, 4).reshape(stations * 2 * FRAMES, 2 * FINE)
    spectra = jnp.dot(frame_rows, fourier_table(FINE), precision=lax.Precision.HIGHEST).astype(
        jnp.bfloat16
    )
    spectra = spectra.reshape(stations, 2, FRAMES, 2, CT, CB)
    return spectra.transpose(4, 1, 0, 3, 2, 5).reshape(CT, 2, stations, 2 * FRAMES * CB)


def grid_body(table, index, urow, lhs, rhs, *rest):
    earlier, (send, keep, vis, taps, amat, wmat) = rest[:-6], rest[-6:]
    step = pl.program_id(0)

    @pl.when(step == 0)
    def _():
        send[...] = earlier[0][...] if earlier else jnp.zeros_like(send)
        keep[...] = earlier[1][...] if earlier else jnp.zeros_like(keep)

    product = lax.dot_general(
        lhs[0], rhs[0], (((1,), (1,)), ((), ())), preferred_element_type=jnp.float32
    )
    product = (product * (1.0 / (FRAMES * CB))).astype(jnp.bfloat16).astype(jnp.float32)
    vis[...] = product.reshape(4, STN_DEV, 2 * PART)
    for axis in range(2):
        chosen = index[0, 3 + axis]
        masks = [chosen == o for o in range(1, OS)]
        for k in range(KW):
            value = jnp.full((STN_DEV, PART), table[0, k], jnp.float32)
            for o in range(1, OS):
                value = jnp.where(masks[o - 1], table[o, k], value)
            taps[axis * KW + k] = value

    def stations(turn, carry):
        for inner in range(BUNCH):
            def pick(ref, lead, lanes=slice(None)):
                low = ref[lead + (slice(inner, inner + 1), lanes)]
                up = ref[lead + (slice(BUNCH + inner, BUNCH + inner + 1), lanes)]
                return jnp.where(turn == 0, low, up)

            lanes = slice(inner * PART, (inner + 1) * PART)
            position = pick(index, (0, 0))
            u0 = pick(index, (0, 1)) + 64 * (position & 1) - KW // 2
            v0 = pick(index, (0, 2)) - KW // 2
            high = position >> 1
            shape = (G, PART)
            away = lax.broadcasted_iota(jnp.int32, shape, 0) - v0
            down = jnp.zeros(shape, jnp.float32)
            for k in range(KW):
                down = jnp.where(away == k, pick(taps, (KW + k,)), down)
            for h in range(NSUB // 2):
                amat[h * G : (h + 1) * G, lanes] = jnp.where(high == h, down, 0.0).astype(
                    jnp.bfloat16
                )
            tap_rows = [pick(taps, (k,)) for k in range(KW)]
            values = [
                pick(vis, (j // 2,), slice((j % 2) * PART, (j % 2 + 1) * PART)) for j in range(8)
            ]
            for half in range(2):
                away = urow[half * G : (half + 1) * G, :] - u0
                across = jnp.zeros(shape, jnp.float32)
                for k in range(KW):
                    across = jnp.where(away == k, tap_rows[k], across)
                for j in range(8):
                    first = half * 8 * G + j * G
                    wmat[first : first + G, lanes] = (values[j] * across).astype(jnp.bfloat16)
        total = lax.dot_general(
            wmat[...], amat[...], (((1,), (1,)), ((), ())), preferred_element_type=jnp.float32
        )
        send[...] += total[: SIDE // 2]
        keep[...] += total[SIDE // 2 :]
        return carry

    lax.fori_loop(0, STN_DEV // BUNCH, stations, 0)


def grid_tiles(table, index, urow, lhs, rhs, earlier, part):
    half = jax.ShapeDtypeStruct((SIDE // 2, SIDE), jnp.float32)
    whole = pl.BlockSpec((SIDE // 2, SIDE), lambda t: (0, 0))
    lanes = 2 * FRAMES * CB
    return pl.pallas_call(
        grid_body,
        grid=(CT,),
        in_specs=[
            pl.BlockSpec(memory_space=pltpu.SMEM),
            pl.BlockSpec((1, 5, STN_DEV, PART), lambda t: (t, 0, 0, part)),
            pl.BlockSpec((2 * G, PART), lambda t: (0, 0)),
            pl.BlockSpec((1, 4 * STN_DEV, lanes), lambda t: (t, 0, 0)),
            pl.BlockSpec((1, 2 * PART, lanes), lambda t: (t, 0, 0)),
        ]
        + [whole] * len(earlier),
        out_specs=[whole, whole],
        out_shape=[half, half],
        input_output_aliases={5: 0, 6: 1} if earlier else {},
        scratch_shapes=[
            pltpu.VMEM((4, STN_DEV, 2 * PART), jnp.float32),
            pltpu.VMEM((2 * KW, STN_DEV, PART), jnp.float32),
            pltpu.VMEM((SIDE, BUNCH * PART), jnp.bfloat16),
            pltpu.VMEM((SIDE, BUNCH * PART), jnp.bfloat16),
        ],
    )(table, index, urow, lhs, rhs, *earlier)


def spread_over_plane(spectra):
    copies = jnp.broadcast_to(spectra, (16,) + spectra.shape)
    pieces = lax.all_to_all(copies, ("x", "y"), 0, 0, tiled=True)
    near = pieces.transpose(1, 2, 0, 3, 4).reshape(CT, 2 * PART, 2 * FRAMES * CB)
    far = lax.ppermute(near, "core", [(0, 1), (1, 0)])
    return [near, far]


def arrival_order():
    slot = jnp.arange(STATIONS, dtype=jnp.int32)
    zh = lax.axis_index("zh") ^ (slot // 256)
    core = lax.axis_index("core") ^ (slot // 128 % 2)
    return ((slot // 8 % 16) * 4 + zh * 2 + core) * STN_DEV + slot % 8


def whole_step(
    voltages, prototype, kernel_table, tile_subgrid, tile_cells, tile_offsets, subgrid_slot
):
    swap = [(0, 1), (1, 0)]
    spectra = channelize(voltages, prototype)
    other = lax.ppermute(spectra, "zh", swap)
    parts = spread_over_plane(spectra)
    lanes = FRAMES * CB
    turned = jnp.concatenate([spectra[..., lanes:], -spectra[..., :lanes]], axis=-1)
    lhs = jnp.stack([spectra, turned], axis=1).reshape(CT, 4 * STN_DEV, 2 * lanes)

    core = lax.axis_index("core")
    subgrid = tile_subgrid.reshape(STN_DEV, CT, STATIONS)
    places = jnp.arange(NSUB, dtype=jnp.int32)
    position = jnp.sum(
        jnp.where(subgrid[..., None] == places, subgrid_slot, 0), axis=-1
    )
    mine = lax.axis_index(STN) * STN_DEV + jnp.arange(STN_DEV, dtype=jnp.int32)
    station = jnp.arange(STATIONS, dtype=jnp.int32)
    position = jnp.where(mine[:, None, None] == station, -1, position)
    cells = tile_cells.reshape(STN_DEV, CT, STATIONS, 2)
    offsets = tile_offsets.reshape(STN_DEV, CT, STATIONS, 2)
    index = jnp.stack(
        [position, cells[..., 0], cells[..., 1], offsets[..., 0], offsets[..., 1]], axis=0
    ).transpose(2, 0, 1, 3)
    chosen = (station[:, None] == arrival_order()[None, :]).astype(jnp.bfloat16)
    index = jnp.dot(
        index.reshape(-1, STATIONS).astype(jnp.bfloat16),
        chosen,
        preferred_element_type=jnp.float32,
    )
    index = index.astype(jnp.int32).reshape(CT, 5, STN_DEV, STATIONS)
    r = jnp.arange(G, dtype=jnp.int32)
    base = (r // 24) * 24 + (r // 12) % 2 * 12 + r % 6 + 64 * ((r // 6) % 2)
    urow = jnp.concatenate([base + 6 * (1 - core), base + 6 * core])
    urow = jnp.broadcast_to(urow[:, None], (2 * G, PART))
    table = lax.reduce_precision(kernel_table, 8, 7)

    other, table, index, urow, lhs = lax.optimization_barrier((other, table, index, urow, lhs))
    parts = parts + spread_over_plane(other)
    grids = ()
    for part, rhs in enumerate(parts):
        grids = grid_tiles(table, index, urow, lhs, rhs, grids, part)
    send, keep = grids
    total = keep + lax.ppermute(send.astype(jnp.bfloat16), "core", swap).astype(jnp.float32)
    total = total.astype(jnp.bfloat16).reshape(16, 24, SIDE)
    total = lax.all_to_all(total, ("x", "y"), 0, 0, tiled=True)
    total = jnp.sum(total.astype(jnp.float32), axis=0)
    total = total.reshape(2, 12, 8, 96).transpose(0, 2, 1, 3).reshape(16, 12, 96)
    total = jnp.sum(lax.all_to_all(total, ("zh", "chan"), 0, 0, tiled=True), axis=0)
    total = total.reshape(2, 6, 2, G)
    return total.transpose(2, 0, 3, 1).reshape(4, G, 6)


def solution(mesh):
    fine = Mesh(mesh.devices.reshape(4, 4, 2, 2, 8), STN + ("chan",))
    return jax.shard_map(
        whole_step,
        mesh=fine,
        in_specs=(
            P(STN, None, None, "chan", None),
            P(),
            P(),
            P("chan", STN, None, None, None),
            P("chan", STN, None, None, None),
            P("chan", STN, None, None, None),
            P(),
        ),
        out_specs=P("chan", None, STN),
        check_vma=False,
    )
```
